256 devices in a mesh: grp: 4 (over y), shard: 64 (over z, x, core).
Axes of the slice: x: 4, y: 4, z: 8, core: 2. Of those that a mesh axis runs over, the one named last changes fastest.
Arguments:
- query_rows: bfloat16 [65536, 1024], P(('grp', 'shard')), may hold values from -6 to 6
- key_rows: bfloat16 [65536, 1024], P(('grp', 'shard')), may hold values from -6 to 6
- value_rows: bfloat16 [65536, 1024], P(('grp', 'shard')), may hold values from -6 to 6
- grad_out: bfloat16 [65536, 1024], P(('grp', 'shard')), may hold values from -6 to 6
Outputs:
- attended: bfloat16 [65536, 1024], P(('grp', 'shard'))
- grad_query: bfloat16 [65536, 1024], P(('grp', 'shard'))
- grad_key: bfloat16 [65536, 1024], P(('grp', 'shard'))
- grad_value: bfloat16 [65536, 1024], P(('grp', 'shard'))
The draws below stay inside these ranges and needn't reach their ends.
All inputs are finite; a program needn't handle non-finite values.
Results may differ from the reference program's by a relative error of at most 0.012.
Values may be sent and summed in bfloat16 or wider, within the bound.
A program may use at most 256 MiB of HBM per device.

```python
import jax
import jax.numpy as jnp
from jax import lax

HEADS = 8
HD = 128
TOK_DEV = 256
TOKENS = 65536


def levels(rng, dims, shards, smallest, top_value):
    loudness = 1.0
    for axis_at, parts in shards:
        draws = jax.random.uniform(jax.random.fold_in(jax.random.fold_in(rng, 6), axis_at), (parts,), jnp.float32, smallest / len(shards), top_value / len(shards))
        loudness = loudness * jnp.repeat(jnp.exp(draws), dims[axis_at] // parts).reshape((-1,) + (1,) * (len(dims) - 1 - axis_at))
    return loudness


def normal_values(stream_key, shape, deviation, limit, shards=(), dtype=jnp.bfloat16):
    result = deviation * jax.random.normal(stream_key, shape, jnp.float32)
    if shards:
        result = result * levels(stream_key, shape, shards, -0.22, 0.18)
    return jnp.clip(result, -limit, limit).astype(dtype)


def setup_inputs(seed: int = 0) -> dict:
    key_list = jax.random.split(jax.random.key(seed), 5)
    return {
        "query_rows": normal_values(key_list[0], (TOKENS, HEADS * HD), 1.0, 6.0, ((0, 256),)),
        "key_rows": normal_values(key_list[1], (TOKENS, HEADS * HD), 1.0, 6.0, ((0, 256),)),
        "value_rows": normal_values(key_list[2], (TOKENS, HEADS * HD), 1.0, 6.0, ((0, 256),)),
        "grad_out": normal_values(key_list[3], (TOKENS, HEADS * HD), 1.0, 6.0, ((0, 256),)),
    }


def rounded(array):
    return lax.optimization_barrier(array.astype(jnp.bfloat16)).astype(jnp.float32)

def causal_mask():
    rows_at = lax.broadcasted_iota(jnp.int32, (TOK_DEV, TOK_DEV), 0)
    cols_at = lax.broadcasted_iota(jnp.int32, (TOK_DEV, TOK_DEV), 1)
    return (rows_at >= cols_at)[None]

def block_scores(query_float, key_float, value_float, grad_float):
    causal = causal_mask()
    scores = jnp.einsum('thd,shd->hts', query_float, key_float)
    local_scores = rounded(jnp.where(causal, scores, 0.0))
    grad_raw = jnp.einsum('the,she->hts', grad_float, value_float)
    grad_scores = rounded(jnp.where(causal, grad_raw, 0.0))
    return (local_scores, grad_scores)

def reference(query_rows, key_rows, value_rows, grad_out):
    seq_len = query_rows.shape[0]
    block_count = seq_len // TOK_DEV

    def split(array):
        return array.reshape(block_count, TOK_DEV, HEADS, HD)
    causal = causal_mask()
    blocks = (split(query_rows), split(key_rows), split(value_rows), split(grad_out))

    def forward_step(carry, pieces):
        query_float = pieces[0].astype(jnp.float32)
        key_float = pieces[1].astype(jnp.float32)
        value_float = pieces[2].astype(jnp.float32)
        grad_float = pieces[3].astype(jnp.float32)
        scores = jnp.einsum('thd,shd->hts', query_float, key_float)
        local_scores = rounded(jnp.where(causal, scores, 0.0))
        block_state = jnp.einsum('thd,the->hde', key_float, value_float)
        earlier_rounded = rounded(carry)
        mixed_rows = jnp.einsum('hts,she->the', local_scores, value_float) + jnp.einsum('thd,hde->the', query_float, earlier_rounded)
        inv_rms = lax.rsqrt(lax.optimization_barrier(jnp.mean(mixed_rows * mixed_rows, axis=-1, keepdims=True)) + 1.0)
        normed = mixed_rows * inv_rms
        attended = normed.astype(jnp.bfloat16)
        grad_mixed = ((grad_float - normed * lax.optimization_barrier(jnp.mean(grad_float * normed, axis=-1, keepdims=True))) * inv_rms).astype(jnp.bfloat16)
        grad_mixed_float = lax.optimization_barrier(grad_mixed).astype(jnp.float32)
        grad_raw = jnp.einsum('the,she->hts', grad_mixed_float, value_float)
        grad_scores = rounded(jnp.where(causal, grad_raw, 0.0))
        grad_query = jnp.einsum('hts,shd->thd', grad_scores, key_float) + jnp.einsum('the,hde->thd', grad_mixed_float, earlier_rounded)
        return (carry + block_state, (attended, grad_query.astype(jnp.bfloat16), grad_mixed))
    start = jnp.zeros((HEADS, HD, HD), jnp.float32)
    unused, outputs = lax.scan(forward_step, start, blocks)
    attended, grad_query, grad_mixed = outputs

    def backward_step(carry, pieces):
        query_float = pieces[0].astype(jnp.float32)
        key_float = pieces[1].astype(jnp.float32)
        value_float = pieces[2].astype(jnp.float32)
        grad_float = pieces[3].astype(jnp.float32)
        local_scores, grad_scores = block_scores(query_float, key_float, value_float, grad_float)
        later_rounded = rounded(carry)
        grad_key = jnp.einsum('hts,thd->shd', grad_scores, query_float) + jnp.einsum('she,hde->shd', value_float, later_rounded)
        grad_value = jnp.einsum('hts,the->she', local_scores, grad_float) + jnp.einsum('shd,hde->she', key_float, later_rounded)
        block_reverse = jnp.einsum('thd,the->hde', query_float, grad_float)
        return (carry + block_reverse, (grad_key.astype(jnp.bfloat16), grad_value.astype(jnp.bfloat16)))
    back_blocks = (blocks[0], blocks[1], blocks[2], grad_mixed)
    unused_back, back_outputs = lax.scan(backward_step, start, back_blocks, reverse=True)
    grad_key, grad_value = back_outputs

    def joined(array):
        return array.reshape(seq_len, HEADS * HD)
    return (joined(attended), joined(grad_query), joined(grad_key), joined(grad_value))
```

```python
import functools

import jax
import jax.numpy as jnp
from jax import lax
from jax.experimental import pallas as pl
from jax.experimental.pallas import tpu as pltpu
from jax.sharding import PartitionSpec as P

HD = 128
ROW = 8
MESH = pl.DeviceIdType.MESH
F32 = jnp.float32
BF16 = jnp.bfloat16


def dot(a, b, ca, cb):
    return lax.dot_general(a, b, (((ca,), (cb,)), ((), ())), preferred_element_type=F32)


def head(ref, h):
    if isinstance(h, int):
        return ref.at[:, h * HD:(h + 1) * HD]
    return ref.at[:, pl.ds(pl.multiple_of(h * HD, HD), HD)]


def scan_kernel(ny, nz, q_ref, k_ref, v_ref, g_ref, att_ref, gq_ref, kl_ref, vl_ref, later_ref,
                ls, lm, gm, s1, r1, ry, ab, rz, s4, r4,
                ss1, rs1, ssy, rsy, ssz, rsz, ss4, rs4):
    y = lax.axis_index("grp")
    shard = lax.axis_index("shard")
    z = shard // ROW
    j = lax.rem(shard, ROW)
    tok = q_ref.shape[0]
    order = (4, 3, 5, 2, 6, 1, 7)

    def in_row(d):
        return lax.rem(j + d, ROW)

    barrier = pltpu.get_barrier_semaphore()
    for d in range(1, ROW):
        pl.semaphore_signal(barrier, inc=1, device_id=(y, z * ROW + in_row(d)), device_id_type=MESH)
    for d in range(1, ny):
        pl.semaphore_signal(barrier, inc=1, device_id=(lax.rem(y + d, ny), shard), device_id_type=MESH)
    for d in range(1, nz):
        pl.semaphore_signal(barrier, inc=1, device_id=(y, lax.rem(z + d, nz) * ROW + j), device_id_type=MESH)

    def to_owner(i, d):
        return pltpu.make_async_remote_copy(
            src_ref=s1.at[i, d], dst_ref=r1.at[i, j], send_sem=ss1.at[i, d], recv_sem=rs1.at[i, d],
            device_id=(y, z * ROW + in_row(d)), device_id_type=MESH)

    def along_y(i, d):
        return pltpu.make_async_remote_copy(
            src_ref=ry.at[i, y], dst_ref=ry.at[i, y], send_sem=ssy.at[i, d], recv_sem=rsy.at[i, d],
            device_id=(lax.rem(y + d, ny), shard), device_id_type=MESH)

    def along_z(i, d):
        there = lax.rem(z + d, nz)
        beyond = (there > z) if i == 0 else (there < z)
        return pltpu.make_async_remote_copy(
            src_ref=ab.at[i, 1 - beyond.astype(jnp.int32)], dst_ref=rz.at[i, d - 1],
            send_sem=ssz.at[i, d], recv_sem=rsz.at[i, d],
            device_id=(y, there * ROW + j), device_id_type=MESH)

    def from_owner(i, d):
        return pltpu.make_async_remote_copy(
            src_ref=s4.at[i, in_row(d)], dst_ref=r4.at[i, j], send_sem=ss4.at[i, d], recv_sem=rs4.at[i, d],
            device_id=(y, z * ROW + in_row(d)), device_id_type=MESH)

    def causal():
        rows_at = lax.broadcasted_iota(jnp.int32, (tok, tok), 0)
        cols_at = lax.broadcasted_iota(jnp.int32, (tok, tok), 1)
        return rows_at >= cols_at

    def middle(i, fill_a, fill_b):
        fill_a()
        for d in order:
            to_owner(i, d).wait_recv()
        total = r1[i, 0].astype(F32)
        for n in range(1, ROW):
            total = total + r1[i, n].astype(F32)
        ry[i, y] = total.astype(BF16)
        for d in range(1, ny):
            along_y(i, d).start()
        for d in range(1, ny):
            along_y(i, d).wait_recv()
        before = jnp.zeros((HD, HD), F32)
        for n in range(ny):
            inside = (n < y) if i == 0 else (n > y)
            before = before + ry[i, n].astype(F32) * inside.astype(F32)
        upto = before + ry[i, y].astype(F32)
        ab[i, 0] = upto.astype(BF16)
        ab[i, 1] = before.astype(BF16)
        for d in (4, 3, 5, 2, 6, 1, 7):
            if d < nz:
                along_z(i, d).start()
        fill_b()
        base = before
        for d in range(1, nz):
            along_z(i, d).wait_recv()
            base = base + rz[i, d - 1].astype(F32)
        for n in (range(ROW) if i == 0 else range(ROW - 1, -1, -1)):
            s4[i, n] = base.astype(BF16)
            base = base + r1[i, n].astype(F32)
        for d in order:
            from_owner(i, d).start()
        r4[i, j] = s4[i, j]

    for d in order:
        h = in_row(d)
        s1[0, d] = dot(head(k_ref, h)[...], head(v_ref, h)[...], 0, 0).astype(BF16)
    pl.semaphore_wait(barrier, ROW - 1 + ny - 1 + nz - 1)
    for d in order:
        to_owner(0, d).start()
    r1[0, j] = dot(head(k_ref, j)[...], head(v_ref, j)[...], 0, 0).astype(BF16)

    def forward_local():
        def one(h, carry):
            scores = dot(head(q_ref, h)[...], head(k_ref, h)[...], 1, 1)
            scores = jnp.where(causal(), scores, 0.0).astype(BF16)
            ls[h] = scores
            lm[h] = dot(scores, head(v_ref, h)[...], 1, 0)
            return carry
        lax.fori_loop(0, ROW, one, 0)

    middle(0, forward_local, lambda: None)

    for d in (0, 1, 7, 2, 6, 3, 5, 4):
        h = in_row(d)
        if d:
            from_owner(0, ROW - d).wait_recv()
        q = head(q_ref, h)[...]
        mixed = lm[h] + dot(q, r4[0, h], 1, 0)
        inv_rms = lax.rsqrt(jnp.mean(mixed * mixed, axis=-1, keepdims=True) + 1.0)
        normed = mixed * inv_rms
        head(att_ref, h)[...] = normed.astype(BF16)
        grad = head(g_ref, h)[...].astype(F32)
        grad_mixed = ((grad - normed * jnp.mean(grad * normed, axis=-1, keepdims=True)) * inv_rms).astype(BF16)
        gm[h] = grad_mixed
        reverse = dot(q, grad_mixed, 0, 0).astype(BF16)
        if d:
            s1[1, d] = reverse
            to_owner(1, d).start()
        else:
            r1[1, j] = reverse

    def backward_local(first, last):
        def one(h, carry):
            grad_mixed = gm[h]
            k = head(k_ref, h)[...]
            scores = dot(grad_mixed, head(v_ref, h)[...], 1, 1)
            scores = jnp.where(causal(), scores, 0.0).astype(BF16)
            query = dot(scores, k, 1, 0) + dot(grad_mixed, r4[0, h], 1, 1)
            head(gq_ref, h)[...] = query.astype(BF16)
            head(kl_ref, h)[...] = dot(scores, head(q_ref, h)[...], 0, 0)
            head(vl_ref, h)[...] = dot(ls[h], grad_mixed, 0, 0)
            return carry
        lax.fori_loop(first, last, one, 0)

    middle(1, lambda: backward_local(0, 4), lambda: backward_local(4, 8))

    for d in order:
        from_owner(1, d).wait_recv()
    later_ref[...] = r4[1]

    for i in range(2):
        for d in order:
            to_owner(i, d).wait_send()
            from_owner(i, d).wait_send()
        for d in range(1, ny):
            along_y(i, d).wait_send()
        for d in range(1, nz):
            along_z(i, d).wait_send()


def final_kernel(k_ref, v_ref, later_ref, kl_ref, vl_ref, a_ref, q_ref, att_ref, gq_ref, gk_ref, gv_ref):
    att_ref[...] = a_ref[...]
    gq_ref[...] = q_ref[...]
    for h in range(ROW):
        later = later_ref[h]
        head(gk_ref, h)[...] = (head(kl_ref, h)[...] + dot(head(v_ref, h)[...], later, 1, 1)).astype(BF16)
        head(gv_ref, h)[...] = (head(vl_ref, h)[...] + dot(head(k_ref, h)[...], later, 1, 0)).astype(BF16)


def body(ny, nz, q, k, v, g):
    tok, width = q.shape
    vmem = pl.BlockSpec(memory_space=pltpu.VMEM)
    rows = jax.ShapeDtypeStruct((tok, width), BF16)
    rows_f32 = jax.ShapeDtypeStruct((tok, width), F32)
    dma = pltpu.SemaphoreType.DMA
    state = lambda n: pltpu.VMEM((2, n, HD, HD), BF16)
    att, gq, kl, vl, later = pl.pallas_call(
        functools.partial(scan_kernel, ny, nz),
        out_shape=(rows, rows, rows_f32, rows_f32, jax.ShapeDtypeStruct((ROW, HD, HD), BF16)),
        in_specs=[vmem] * 4,
        out_specs=(vmem,) * 5,
        scratch_shapes=[
            pltpu.VMEM((ROW, tok, tok), BF16),
            pltpu.VMEM((ROW, tok, HD), F32),
            pltpu.VMEM((ROW, tok, HD), BF16),
            state(ROW), state(ROW), state(ny), state(2), state(nz), state(ROW), state(ROW),
            dma((2, ROW)), dma((2, ROW)), dma((2, ny)), dma((2, ny)),
            dma((2, nz)), dma((2, nz)), dma((2, ROW)), dma((2, ROW)),
        ],
        compiler_params=pltpu.CompilerParams(collective_id=0, has_side_effects=True),
        name="scan",
    )(q, k, v, g)
    tile = tok // 2
    narrow = pl.BlockSpec((tile, width), lambda i: (i, 0))
    whole = pl.BlockSpec((ROW, HD, HD), lambda i: (0, 0, 0))
    return pl.pallas_call(
        final_kernel,
        grid=(2,),
        out_shape=(rows,) * 4,
        in_specs=[narrow, narrow, whole, narrow, narrow, narrow, narrow],
        out_specs=(narrow,) * 4,
        name="final",
    )(k, v, later, kl, vl, att, gq)


def solution(mesh):
    ny = mesh.shape["grp"]
    nz = mesh.shape["shard"] // ROW
    spec = P(("grp", "shard"), None)
    return jax.shard_map(functools.partial(body, ny, nz), mesh=mesh, in_specs=(spec,) * 4,
                         out_specs=(spec,) * 4, check_vma=False)
```
